128 devices in a mesh: row: 8 (over z, x_hi), col: 16 (over x_lo, y, core).
Axes of the slice: x: 4 (x_hi: 2, x_lo: 2; x = x_hi * 2 + x_lo), y: 4, z: 4, core: 2. Of those that a mesh axis runs over, the one named last changes fastest.
Arguments:
- eigvecs: bfloat16 [81920, 4096], P('row', 'col'), may hold values from -0.09375 to 0.09375
- reflectors: bfloat16 [2, 81920, 128], P(None, 'row'), may hold values from -6 to 6
- factors: float32 [2, 128, 128], replicated, may hold values from -0.00015258789 to 0.00015258789
- frequencies: float32 [4096], replicated, may hold values from 0.3 to 3
- region_blocks: int32 [72], P('row'), may hold values from 0 to 639, as said below
Outputs:
- covariance: float32 [9216, 9216], P('row', 'col')
The draws below stay inside these ranges and needn't reach their ends.
Inputs may be any that keep to these rules, and one draw needn't show every extreme that they name: `region_blocks`: the 72 block numbers are distinct and ascending; exactly 9 of them lie in each consecutive run of 80 block numbers.
All inputs are finite; a program needn't handle non-finite values.
Results may differ from the reference program's by a relative error of at most 0.004.
Values may be sent and summed in bfloat16 or wider, within the bound.
No kernel may reach another device: no remote copies, remote signals or barrier semaphores. Data moves between devices by JAX's collectives and lax.ppermute only.
A program may use at most 128 MiB of HBM per device.

```python
import math
import jax
import jax.numpy as jnp
from jax import lax

ROWS_DEV = 10240
HB = 128
BLOCK = 128
N = 81920
K = 4096
RBD = 9
N_ROW = 8


def draw_region_blocks(key, part):
    local_blocks = ROWS_DEV // BLOCK
    scores = jax.random.randint(key, (N_ROW, local_blocks), 0, 1 << 20)
    scores = scores * local_blocks + jnp.arange(local_blocks, dtype=jnp.int32)[None, :]
    chosen = lax.top_k(scores, RBD)[1]
    chosen = jnp.sort(chosen, axis=1)
    chosen = chosen + jnp.arange(N_ROW, dtype=jnp.int32)[:, None] * local_blocks
    return chosen.reshape(-1).astype(jnp.int32)


def level_of(key, shape, pieces, low, top_value):
    level = 1.0
    for axis_at, blocks in pieces:
        draws = jax.random.uniform(jax.random.fold_in(jax.random.fold_in(key, 6), axis_at), (blocks,), jnp.float32, low / len(pieces), top_value / len(pieces))
        level = level * jnp.repeat(jnp.exp(draws), shape[axis_at] // blocks).reshape((-1,) + (1,) * (len(shape) - 1 - axis_at))
    return level


def scatter_about(own_key, shape, spread, reach, pieces=(), kind=jnp.bfloat16):
    array = jax.random.normal(own_key, shape, jnp.float32) * spread
    if len(pieces) > 0:
        array = level_of(own_key, shape, pieces, -0.22, 0.18) * array
    return jnp.clip(array, min=-reach, max=reach).astype(kind)


def setup_inputs(seed: int = 0) -> dict:
    seeds = jax.random.split(jax.random.key(seed), 6)
    return {
        "eigvecs": scatter_about(seeds[0], (N, K), K ** -0.5, 0.09375, ((0, 8), (1, 16))),
        "reflectors": scatter_about(seeds[1], (2, N, HB), 1.0, 6.0, ((1, 8),)),
        "factors": scatter_about(seeds[2], (2, HB, HB), (HB * HB * N) ** -0.5, 0.00015258789, (), jnp.float32),
        "frequencies": jnp.clip(jnp.exp(jax.random.uniform(seeds[3], (K,), jnp.float32, math.log(0.3), math.log(3.0))), 0.3, 3.0),
        "region_blocks": draw_region_blocks(jax.random.fold_in(seeds[5], 71), 0),
    }


def contract_rows(left, right):
    return lax.dot_general(left, right, (((0,), (0,)), ((), ())), preferred_element_type=jnp.float32)


def reference(eigvecs, reflectors, factors, frequencies, region_blocks):
    first_block = reflectors[0]
    second_block = reflectors[1]
    first_factor = jnp.triu(factors[0])
    second_factor = jnp.triu(factors[1])
    highest = lax.Precision.HIGHEST
    second_proj = contract_rows(second_block, eigvecs)
    second_apply = jnp.dot(second_factor, second_proj, precision=highest).astype(jnp.bfloat16)
    cross = contract_rows(first_block, second_block)
    first_proj = contract_rows(first_block, eigvecs) - jnp.dot(cross, second_apply.astype(jnp.float32), precision=highest)
    first_apply = jnp.dot(first_factor, first_proj, precision=highest).astype(jnp.bfloat16)
    offsets = jnp.arange(BLOCK, dtype=jnp.int32)
    rows = (region_blocks.astype(jnp.int32)[:, None] * BLOCK + offsets[None, :]).reshape(-1)
    region = eigvecs[rows].astype(jnp.float32)
    region = region - jnp.dot(second_block[rows], second_apply, preferred_element_type=jnp.float32)
    region = region - jnp.dot(first_block[rows], first_apply, preferred_element_type=jnp.float32)
    region = region.astype(jnp.bfloat16)
    weight = 1.0 / jnp.tanh(frequencies / 2.0) / (2.0 * frequencies)
    scaled = (region.astype(jnp.float32) * weight[None, :]).astype(jnp.bfloat16)
    return lax.dot_general(scaled, region, (((1,), (1,)), ((), ())), preferred_element_type=jnp.float32)
```

```python
import jax
import jax.numpy as jnp
from jax import lax
from jax.experimental import pallas as pl
from jax.experimental.pallas import tpu as pltpu
from jax.sharding import Mesh, PartitionSpec as P

BLOCK = 128
F32 = jnp.float32
BF16 = jnp.bfloat16
ALL = ("z", "xh", "xl", "y", "core")
NZ, NX, NL, NY, NC = 4, 2, 2, 4, 2


def shift(x, axis, size, step):
    return lax.ppermute(x, axis, [(i, (i + step) % size) for i in range(size)])


def flip(x, axis, size, bit):
    return lax.ppermute(x, axis, [(i, i ^ bit) for i in range(size)])


def place(z, xh, xl, y, k):
    return (((z * NX + xh) * NL + xl) * NY + y) * NC + k


def turn_pairs():
    pairs = []
    for z in range(NZ):
        for xh in range(NX):
            for xl in range(NL):
                for y in range(NY):
                    to = ((z + y) % NZ, xh ^ xl ^ (z >> 1), z >> 1, 2 * (z & 1) + xh)
                    for k in range(NC):
                        pairs.append((place(z, xh, xl, y, k), place(*to, k)))
    return pairs


def first_dims(left, right):
    return lax.dot_general(
        left, right, (((0,), (0,)), ((), ())), preferred_element_type=F32
    )


def last_dims(left, right):
    return lax.dot_general(
        left, right, (((1,), (1,)), ((), ())), preferred_element_type=F32
    )


def last_dims_exact(left, right):
    return lax.dot_general(
        left,
        right,
        (((1,), (1,)), ((), ())),
        precision=lax.Precision.HIGHEST,
        preferred_element_type=F32,
    )


STEPS = 4


def head_kernel(
    index,
    coords,
    vecs_block,
    refl_block,
    eigvecs,
    reflectors,
    keep,
    send,
    own,
    carry,
    turned,
    refl,
    sums,
    cross,
    own_v,
    refl_v,
    sem_in,
    sem_out,
):
    step = pl.program_id(0)
    rows, width = own_v.shape[0], reflectors.shape[2]
    share = turned.shape[0] - rows
    loads = []
    for i in range(rows // BLOCK):
        take = pl.ds(pl.multiple_of(index[i] * BLOCK, BLOCK), BLOCK)
        to = pl.ds(i * BLOCK, BLOCK)
        loads.append((eigvecs.at[take], own_v.at[to]))
        for n in range(2):
            loads.append(
                (reflectors.at[n, take], refl_v.at[to, pl.ds(n * width, width)])
            )
    loads = [
        pltpu.make_async_copy(a, b, sem_in.at[n]) for n, (a, b) in enumerate(loads)
    ]
    part = pl.ds(pl.multiple_of((coords[2] * NY + coords[3]) * share, 16), share)
    stores = [
        (own_v, own),
        (own_v, carry.at[pl.ds(0, rows)]),
        (own_v, turned.at[pl.ds(0, rows)]),
        (refl_v.at[part], turned.at[pl.ds(rows, share)]),
        (refl_v, refl),
    ]
    stores = [
        pltpu.make_async_copy(a, b, sem_out.at[n]) for n, (a, b) in enumerate(stores)
    ]

    @pl.when(step == 0)
    def _():
        for copy in loads:
            copy.start()
        sums[...] = jnp.zeros_like(sums)
        cross[...] = jnp.zeros_like(cross)

    both = jnp.concatenate([refl_block[0], refl_block[1]], axis=1)
    sums[...] += first_dims(vecs_block[...], both)
    cross[...] += first_dims(refl_block[1], refl_block[0])

    @pl.when(step == 1)
    def _():
        for copy in loads:
            copy.wait()
        for copy in stores:
            copy.start()

    @pl.when(step == STEPS - 1)
    def _():
        half = sums.shape[0] // 2
        mine = coords[0] & 1
        wide = jnp.concatenate([cross[:64, :], cross[64:, :]], axis=1)
        keep[:half, :] = sums[pl.ds(pl.multiple_of(mine * half, half), half), :]
        keep[half:, :] = wide
        send[:half, :] = sums[pl.ds(pl.multiple_of((1 - mine) * half, half), half), :]
        send[half:, :] = wide
        for copy in stores:
            copy.wait()


def head(index, coords, eigvecs, reflectors):
    rows = index.shape[0] * BLOCK
    local, columns = eigvecs.shape
    width = reflectors.shape[2]
    block = local // STEPS
    smem = pl.BlockSpec(memory_space=pltpu.SMEM)
    hbm = pl.BlockSpec(memory_space=pltpu.HBM)
    fixed = pl.BlockSpec((192, 256), lambda i: (0, 0))
    return pl.pallas_call(
        head_kernel,
        grid=(STEPS,),
        in_specs=[
            smem,
            smem,
            pl.BlockSpec((block, columns), lambda i: (i, 0)),
            pl.BlockSpec((2, block, width), lambda i: (0, i, 0)),
            hbm,
            hbm,
        ],
        out_specs=[fixed, fixed] + [hbm] * 4,
        out_shape=[
            jax.ShapeDtypeStruct((192, 256), F32),
            jax.ShapeDtypeStruct((192, 256), F32),
            jax.ShapeDtypeStruct((rows, columns), BF16),
            jax.ShapeDtypeStruct((rows + 256, columns), BF16),
            jax.ShapeDtypeStruct((rows + rows // 8, columns), BF16),
            jax.ShapeDtypeStruct((rows, 2 * width), BF16),
        ],
        scratch_shapes=[
            pltpu.VMEM((256, 256), F32),
            pltpu.VMEM((128, 128), F32),
            pltpu.VMEM((rows, columns), BF16),
            pltpu.VMEM((rows, 2 * width), BF16),
            pltpu.SemaphoreType.DMA((3 * index.shape[0],)),
            pltpu.SemaphoreType.DMA((5,)),
        ],
        compiler_params=pltpu.CompilerParams(vmem_limit_bytes=32 * 2**20),
        name="head",
    )(index, coords, eigvecs, reflectors, eigvecs, reflectors)


def source_of(z, xh, xl, y, dxh, dz):
    zz = lax.rem(z + dz, NZ)
    xx = jnp.bitwise_xor(xh, dxh)
    from_y = lax.rem(zz - (2 * xl + (y >> 1)) + NZ, NZ)
    from_l = jnp.bitwise_xor(jnp.bitwise_xor(xx, y & 1), xl)
    return from_y, from_l


def final_kernel(slots_a, slots_b, coords, weight, ya, *rest):
    a_refs, rest = rest[: len(slots_a)], rest[len(slots_a) :]
    b_refs, rest = rest[: len(slots_b)], rest[len(slots_b) :]
    other, own, c_other, c_own, a_all, b_all, b_raw, yb, p_raw, p_all = rest[:10]
    sem_a, sem_b, sem_y, sem_p, sem_c = rest[10:]
    z, xh, xl, y, k = (coords[i] for i in range(5))
    rows = ya.shape[0]
    share = rows // 8
    copies_b, copies_a, copies_p = [], [], []
    for n, ((dxh, dz, start), ref) in enumerate(zip(slots_b, b_refs)):
        count = min(ref.shape[0], rows - start)
        copies_b.append(
            pltpu.make_async_copy(
                ref.at[pl.ds(0, count)],
                b_raw.at[dxh * NZ + dz, pl.ds(start, count)],
                sem_b.at[n],
            )
        )
        if count < ref.shape[0]:
            from_y, from_l = source_of(z, xh, xl, y, dxh, dz)
            to = pl.multiple_of((from_l * NY + from_y) * share, 16)
            copies_b.append(
                pltpu.make_async_copy(
                    ref.at[pl.ds(count, share)], yb.at[pl.ds(to, share)], sem_y.at[n]
                )
            )
    for n, ((slot, start), ref) in enumerate(zip(slots_a, a_refs)):
        count = min(ref.shape[0], rows - start)
        copies_a.append(
            pltpu.make_async_copy(
                ref.at[pl.ds(0, count)],
                a_all.at[pl.ds(start, count), pl.ds(slot * 256, 256)],
                sem_a.at[n],
            )
        )
        if count < ref.shape[0]:
            copies_p.append(
                pltpu.make_async_copy(
                    ref.at[pl.ds(count, 256)], p_raw.at[slot], sem_p.at[n]
                )
            )
    for copy in copies_p + copies_b + copies_a:
        copy.start()
    for copy in copies_p:
        copy.wait()

    def order(slot, carry):
        for dxh in range(NX):
            for dz in range(NZ):
                zz = lax.rem(z + dz, NZ)
                xx = jnp.bitwise_xor(xh, dxh)
                sub = (zz & 1) * 4 + xx * 2 + (zz >> 1)
                start = pl.multiple_of(slot * 256 + sub * 32, 32)
                chunk = (dxh * NZ + dz) * 32
                p_all[pl.ds(start, 32), :] = p_raw[slot, chunk : chunk + 32, :]
        return carry

    lax.fori_loop(0, NL * NY, order, 0)
    for copy in copies_b:
        copy.wait()

    def back_b(p, carry):
        from_y, from_l = source_of(z, xh, xl, y, p // NZ, p % NZ)
        dx = jnp.bitwise_xor(from_l, xl)
        slot = dx * NY + lax.rem(from_y - y + NY, NY)
        whole = (from_l * NY + from_y) * NC + k
        start = pl.multiple_of(slot * 256, 256)
        value = b_raw[p].astype(F32) - last_dims(yb[...], p_all[pl.ds(start, 256), :])
        value = value * weight[pl.ds(whole, 1), :]
        b_all[:, pl.ds(start, 256)] = value.astype(BF16)
        return carry

    lax.fori_loop(0, NX * NZ, back_b, 0)
    for copy in copies_a:
        copy.wait()

    def back_a(slot, carry):
        cols = pl.ds(pl.multiple_of(slot * 256, 256), 256)
        value = a_all[:, cols].astype(F32) - last_dims(ya[...], p_all[cols, :])
        a_all[:, cols] = value.astype(BF16)
        return carry

    lax.fori_loop(0, NL * NY, back_a, 0)
    half = c_own.shape[1]

    def product(which):
        return last_dims(
            a_all[...], b_all[pl.ds(pl.multiple_of(which * half, half), half), :]
        )

    c_other[...] = product(1 - k).astype(BF16)
    out = [
        pltpu.make_async_copy(c_other, other, sem_c.at[0]),
        pltpu.make_async_copy(c_own, own, sem_c.at[1]),
    ]
    out[0].start()
    c_own[...] = product(k)
    out[1].start()
    out[0].wait()
    out[1].wait()


def final(coords, weight, ya, a_list, b_list):
    slots_a = [s for s, _ in a_list]
    slots_b = [s for s, _ in b_list]
    smem = pl.BlockSpec(memory_space=pltpu.SMEM)
    vmem = pl.BlockSpec(memory_space=pltpu.VMEM)
    hbm = pl.BlockSpec(memory_space=pltpu.HBM)
    rows = ya.shape[0]
    half = rows // 2
    slots = NL * NY

    def body(*refs):
        final_kernel(slots_a, slots_b, *refs)

    other, own = pl.pallas_call(
        body,
        out_shape=[
            jax.ShapeDtypeStruct((rows, half), BF16),
            jax.ShapeDtypeStruct((rows, half), F32),
        ],
        in_specs=[smem, vmem, vmem] + [hbm] * (len(a_list) + len(b_list)),
        out_specs=[hbm, hbm],
        scratch_shapes=[
            pltpu.VMEM((rows, half), BF16),
            pltpu.VMEM((rows, half), F32),
            pltpu.VMEM((rows, 256 * slots), BF16),
            pltpu.VMEM((rows, 256 * slots), BF16),
            pltpu.VMEM((slots, rows, 256), BF16),
            pltpu.VMEM((rows, 256), BF16),
            pltpu.VMEM((slots, 256, 256), BF16),
            pltpu.VMEM((256 * slots, 256), BF16),
            pltpu.SemaphoreType.DMA((len(a_list),)),
            pltpu.SemaphoreType.DMA((len(b_list),)),
            pltpu.SemaphoreType.DMA((len(b_list),)),
            pltpu.SemaphoreType.DMA((len(a_list),)),
            pltpu.SemaphoreType.DMA((2,)),
        ],
        compiler_params=pltpu.CompilerParams(vmem_limit_bytes=48 * 2**20),
        name="covariance",
    )(coords, weight, ya, *[v for _, v in a_list], *[v for _, v in b_list])
    return own + flip(other, "core", NC, 1).astype(F32)


def halve(both, mine):
    half = (both.shape[0] - 64) // 2
    cross = both[2 * half :]
    keep = lax.dynamic_slice_in_dim(both, mine * half, half, 0)
    send = lax.dynamic_slice_in_dim(both, (1 - mine) * half, half, 0)
    return jnp.concatenate([keep, cross], axis=0), jnp.concatenate([send, cross], axis=0)


def apply_factors(both, factors):
    part, cross = both[:32], both[32:]
    cross = jnp.concatenate([cross[:, :128], cross[:, 128:]], axis=0)
    t1, t2 = jnp.triu(factors[0]), jnp.triu(factors[1])
    second_apply = last_dims_exact(part[:, 128:], t2).astype(BF16)
    first_part = part[:, :128] - jnp.dot(
        second_apply.astype(F32), cross, precision=lax.Precision.HIGHEST
    )
    first_apply = last_dims_exact(first_part, t1).astype(BF16)
    return jnp.concatenate([first_apply, second_apply], axis=1)


def ahead(x, axis, size):
    return [x, shift(x, axis, size, -1), shift(x, axis, size, 2), shift(x, axis, size, 1)]


def per_device(eigvecs, reflectors, factors, frequencies, region_blocks):
    z, xh, xl, y, k = (lax.axis_index(a) for a in ALL)
    local_blocks = eigvecs.shape[0] // BLOCK
    index = region_blocks - (z * NX + xh) * local_blocks
    coords = jnp.stack([z, xh, xl, y, k]).astype(jnp.int32)
    keep, send, own, carry, turned, refl = head(index, coords, eigvecs, reflectors)
    rows = own.shape[0]
    mid, low = rows // 2, turned.shape[0] // 32 * 16 + 16
    together = lax.optimization_barrier

    a, b = {}, {}
    b[0, 0] = lax.ppermute(turned, ALL, turn_pairs())
    across = flip(own, "xl", NL, 1)
    both = keep + flip(send, "z", NZ, 1)
    keep, send = halve(both, xh)
    both = keep + flip(send, "xh", NX, 1)
    keep, send = halve(both, z >> 1)
    both = keep + flip(send, "z", NZ, 2)
    p = apply_factors(both, factors)
    p = jnp.concatenate(ahead(p, "z", NZ), axis=0)
    p = jnp.concatenate([p, flip(p, "xh", NX, 1)], axis=0)

    b[0, 0], across, p = together((b[0, 0], across, p))
    a[0, 0] = lax.dynamic_update_slice(carry, p, (rows, 0))
    b[0, 1] = shift(b[0, 0], "z", NZ, -1)
    b[0, 3] = shift(b[0, 0], "z", NZ, 1)
    b[1, 0] = flip(b[0, 0], "xh", NX, 1)
    a[0, 1] = shift(a[0, 0], "y", NY, -1)
    a[0, 3] = shift(a[0, 0], "y", NY, 1)
    a[1, 0] = jnp.concatenate([across, flip(p, "xl", NL, 1)], axis=0)

    a[1, 0], a[0, 1], a[0, 3], b[0, 1], b[0, 3], b[1, 0] = together(
        (a[1, 0], a[0, 1], a[0, 3], b[0, 1], b[0, 3], b[1, 0])
    )
    b[1, 1] = shift(b[1, 0], "z", NZ, -1)
    b[1, 3] = shift(b[1, 0], "z", NZ, 1)
    b02 = [shift(b[0, 1][:low], "z", NZ, -1), shift(b[0, 3][low:], "z", NZ, 1)]
    a[0, 2] = shift(a[0, 1], "y", NY, -1)
    a[1, 3] = shift(a[1, 0], "y", NY, 1)
    a[1, 1] = flip(a[0, 1], "xl", NL, 1)

    a[0, 2], a[1, 3], a[1, 1], b[1, 1], b[1, 3], *b02 = together(
        (a[0, 2], a[1, 3], a[1, 1], b[1, 1], b[1, 3], *b02)
    )
    a12 = [shift(a[1, 1][:mid], "y", NY, -1), shift(a[1, 3][mid:], "y", NY, 1)]
    b12 = [shift(b[1, 1][:low], "z", NZ, -1), shift(b[1, 3][low:], "z", NZ, 1)]

    a_list = [((dx * NY + dy, 0), v) for (dx, dy), v in a.items()]
    a_list += [((NY + 2, 0), a12[0]), ((NY + 2, mid), a12[1])]
    b_list = [((dx, dz, 0), v) for (dx, dz), v in b.items()]
    for dx, (top, rest) in enumerate((b02, b12)):
        b_list += [((dx, 2, 0), top), ((dx, 2, low), rest)]
    weight = 1.0 / jnp.tanh(frequencies / 2.0) / (2.0 * frequencies)
    return final(coords, weight.reshape(16, 256), refl, a_list, b_list)


def solution(mesh):
    grid = Mesh(mesh.devices.reshape(NZ, NX, NL, NY, NC), ALL)
    row, col = ("z", "xh"), ("xl", "y", "core")
    return jax.shard_map(
        per_device,
        mesh=grid,
        in_specs=(P(row, col), P(None, row, None), P(), P(), P(row)),
        out_specs=P(row, col),
        check_vma=False,
    )
```

```python
import jax
import jax.numpy as jnp
from jax import lax
from jax.experimental import pallas as pl
from jax.experimental.pallas import tpu as pltpu
from jax.sharding import Mesh, PartitionSpec as P

BLOCK = 128
F32 = jnp.float32
BF16 = jnp.bfloat16
ALL = ("z", "xh", "xl", "y", "core")
NZ, NX, NL, NY, NC = 4, 2, 2, 4, 2


def shift(x, axis, size, step):
    return lax.ppermute(x, axis, [(i, (i + step) % size) for i in range(size)])


def flip(x, axis, size, bit):
    return lax.ppermute(x, axis, [(i, i ^ bit) for i in range(size)])


def place(z, xh, xl, y, k):
    return (((z * NX + xh) * NL + xl) * NY + y) * NC + k


def turn_pairs():
    pairs = []
    for z in range(NZ):
        for xh in range(NX):
            for xl in range(NL):
                for y in range(NY):
                    turn = 2 * (z & 1) + xh
                    to = (
                        (z - y + turn) % NZ,
                        xh ^ xl ^ (z >> 1) ^ (y & 1),
                        z >> 1,
                        turn,
                    )
                    for k in range(NC):
                        pairs.append((place(z, xh, xl, y, k), place(*to, k)))
    return pairs


def first_dims(left, right):
    return lax.dot_general(
        left, right, (((0,), (0,)), ((), ())), preferred_element_type=F32
    )


def last_dims(left, right):
    return lax.dot_general(
        left, right, (((1,), (1,)), ((), ())), preferred_element_type=F32
    )


def last_dims_exact(left, right):
    return lax.dot_general(
        left,
        right,
        (((1,), (1,)), ((), ())),
        precision=lax.Precision.HIGHEST,
        preferred_element_type=F32,
    )


STEPS = 4


def head_kernel(
    index,
    coords,
    vecs_block,
    refl_block,
    eigvecs,
    reflectors,
    keep,
    send_1,
    send_2,
    send_3,
    own,
    turned,
    refl,
    sums,
    cross,
    sem,
    sem_refl,
):
    step = pl.program_id(0)
    rows, width = own.shape[0], reflectors.shape[2]
    share = turned.shape[0] - rows
    copies, copies_refl = [], []
    for i in range(rows // BLOCK):
        take = pl.ds(pl.multiple_of(index[i] * BLOCK, BLOCK), BLOCK)
        to = pl.ds(i * BLOCK, BLOCK)
        for n, out in enumerate((own, turned)):
            copies.append(
                pltpu.make_async_copy(eigvecs.at[take], out.at[to], sem.at[2 * i + n])
            )
        for n in range(2):
            copies_refl.append(
                pltpu.make_async_copy(
                    reflectors.at[n, take],
                    refl.at[to, pl.ds(n * width, width)],
                    sem_refl.at[2 * i + n],
                )
            )

    @pl.when(step == 0)
    def _():
        for copy in copies_refl + copies:
            copy.start()
        sums[...] = jnp.zeros_like(sums)
        cross[...] = jnp.zeros_like(cross)

    both = jnp.concatenate([refl_block[0], refl_block[1]], axis=1)
    sums[...] += first_dims(vecs_block[...], both)
    cross[...] += first_dims(refl_block[1], refl_block[0])

    @pl.when(step == STEPS - 1)
    def _():
        part = sums.shape[0] // NZ
        wide = jnp.concatenate([cross[:part, :], cross[part:, :]], axis=1)
        for n, out in enumerate((keep, send_1, send_2, send_3)):
            to = lax.rem(coords[0] + n, NZ)
            out[:part, :] = sums[pl.ds(pl.multiple_of(to * part, part), part), :]
            out[part:, :] = wide
        for copy in copies_refl:
            copy.wait()
        start = pl.multiple_of((coords[2] * NY + coords[3]) * share, 16)
        for copy in copies:
            copy.wait()
        turned[rows:, :] = refl[pl.ds(start, share), :]


def head(index, coords, eigvecs, reflectors):
    rows = index.shape[0] * BLOCK
    local, columns = eigvecs.shape
    width = reflectors.shape[2]
    block = local // STEPS
    smem = pl.BlockSpec(memory_space=pltpu.SMEM)
    vmem = pl.BlockSpec(memory_space=pltpu.VMEM)
    hbm = pl.BlockSpec(memory_space=pltpu.HBM)
    sums = jax.ShapeDtypeStruct((128, 256), F32)
    return pl.pallas_call(
        head_kernel,
        grid=(STEPS,),
        in_specs=[
            smem,
            smem,
            pl.BlockSpec((block, columns), lambda i: (i, 0)),
            pl.BlockSpec((2, block, width), lambda i: (0, i, 0)),
            hbm,
            hbm,
        ],
        out_specs=[vmem] * 7,
        out_shape=[sums] * 4
        + [
            jax.ShapeDtypeStruct((rows, columns), BF16),
            jax.ShapeDtypeStruct((rows + rows // 8, columns), BF16),
            jax.ShapeDtypeStruct((rows, 2 * width), BF16),
        ],
        scratch_shapes=[
            pltpu.VMEM((256, 256), F32),
            pltpu.VMEM((128, 128), F32),
            pltpu.SemaphoreType.DMA((2 * index.shape[0],)),
            pltpu.SemaphoreType.DMA((2 * index.shape[0],)),
        ],
        compiler_params=pltpu.CompilerParams(vmem_limit_bytes=20 * 2**20),
        name="head",
    )(
        index,
        coords,
        *[pltpu.with_memory_space_constraint(v, pltpu.HBM) for v in (eigvecs, reflectors)] * 2,
    )


def source_of(z, xh, xl, y, dxh, dz):
    zz = lax.rem(z + dz, NZ)
    from_y = lax.rem(2 * xl + (y >> 1) + y - zz + NZ, NZ)
    from_l = (xh + dxh + (y & 1) + xl + (from_y & 1)) & 1
    return from_y, from_l


def weigh(freqs):
    return 1.0 / jnp.tanh(freqs / 2.0) / (2.0 * freqs)


def final_kernel(slots_a, slots_b, coords, freqs, ya, *rest):
    a_refs, rest = rest[: len(slots_a)], rest[len(slots_a) :]
    b_refs, rest = rest[: len(slots_b)], rest[len(slots_b) :]
    c_other, c_own, a_all, b_all, yb, p_all = rest
    z, xh, xl, y, k = (coords[i] for i in range(5))
    rows = ya.shape[0]
    share = rows // 8

    for (slot, (first, _)), ref in zip(slots_a, a_refs):
        for dz in range(NZ):
            for dxh in range(NX):
                zz = lax.rem(z + dz, NZ)
                xx = jnp.bitwise_xor(xh, dxh)
                to = pl.multiple_of(slot * 256 + (zz * NX + xx) * 32, 32)
                chunk = first + rows + (dz * NX + dxh) * 32
                p_all[pl.ds(to, 32), :] = ref[chunk : chunk + 32, :]
    for ((dxh, dz), (first, _)), ref in zip(slots_b, b_refs):
        from_y, from_l = source_of(z, xh, xl, y, dxh, dz)
        to = pl.multiple_of((from_l * NY + from_y) * share, 16)
        yb[pl.ds(to, share), :] = ref[first + rows : first + rows + share, :]

    for ((dxh, dz), (first, _)), ref in zip(slots_b, b_refs):
        from_y, from_l = source_of(z, xh, xl, y, dxh, dz)
        dx = jnp.bitwise_xor(from_l, xl)
        slot = dx * NY + lax.rem(from_y - y + NY, NY)
        whole = (from_l * NY + from_y) * NC + k
        at = pl.multiple_of(slot * 256, 256)
        value = ref[first : first + rows, :].astype(F32) - last_dims(
            yb[...], p_all[pl.ds(at, 256), :]
        )
        value = value * weigh(
            jnp.concatenate(
                [freqs[pl.ds(2 * whole, 1), :], freqs[pl.ds(2 * whole + 1, 1), :]],
                axis=1,
            )
        )
        b_all[:, pl.ds(at, 256)] = value.astype(BF16)
    for (slot, (first, _)), ref in zip(slots_a, a_refs):
        cols = slice(slot * 256, slot * 256 + 256)
        value = ref[first : first + rows, :].astype(F32) - last_dims(
            ya[...], p_all[cols, :]
        )
        a_all[:, cols] = value.astype(BF16)
    half = c_own.shape[0]

    def product(which):
        return last_dims(
            b_all[pl.ds(pl.multiple_of(which * half, half), half), :], a_all[...]
        )

    c_other[...] = product(1 - k).astype(BF16)
    c_own[...] = product(k)


def add_kernel(own, other, out):
    rows = out.shape[0]
    at = pl.ds(pl.multiple_of(pl.program_id(0) * rows, rows), rows)
    out[...] = own[at, :] + other[at, :].astype(F32)


def final(coords, freqs, ya, a_list, b_list):
    slots_a = [(s, take) for s, take, _ in a_list]
    slots_b = [(s, take) for s, take, _ in b_list]
    smem = pl.BlockSpec(memory_space=pltpu.SMEM)
    vmem = pl.BlockSpec(memory_space=pltpu.VMEM)
    rows = ya.shape[0]
    half = rows // 2
    depth = 256 * NL * NY

    def body(*refs):
        final_kernel(slots_a, slots_b, *refs)

    other, own = pl.pallas_call(
        body,
        out_shape=[
            jax.ShapeDtypeStruct((half, rows), BF16),
            jax.ShapeDtypeStruct((half, rows), F32),
        ],
        in_specs=[smem, vmem, vmem] + [vmem] * (len(a_list) + len(b_list)),
        out_specs=[vmem, vmem],
        scratch_shapes=[
            pltpu.VMEM((rows, depth), BF16),
            pltpu.VMEM((rows, depth), BF16),
            pltpu.VMEM((rows, 256), BF16),
            pltpu.VMEM((depth, 256), BF16),
        ],
        compiler_params=pltpu.CompilerParams(vmem_limit_bytes=24 * 2**20),
        name="covariance",
    )(coords, freqs, ya, *[v for _, _, v in a_list], *[v for _, _, v in b_list])
    got = flip(other, "core", NC, 1)
    return pl.pallas_call(
        add_kernel,
        grid=(4,),
        in_specs=[vmem, vmem],
        out_specs=pl.BlockSpec((half // 4, rows), lambda i: (i, 0)),
        out_shape=jax.ShapeDtypeStruct((half, rows), F32),
        compiler_params=pltpu.CompilerParams(vmem_limit_bytes=4 * 2**20),
        name="add",
    )(own, got).T


def apply_factors(both, factors):
    part, cross = both[:32], both[32:]
    cross = jnp.concatenate([cross[:, :128], cross[:, 128:]], axis=0)
    t1, t2 = jnp.triu(factors[0]), jnp.triu(factors[1])
    second_apply = last_dims_exact(part[:, 128:], t2).astype(BF16)
    first_part = part[:, :128] - jnp.dot(
        second_apply.astype(F32), cross, precision=lax.Precision.HIGHEST
    )
    first_apply = last_dims_exact(first_part, t1).astype(BF16)
    return jnp.concatenate([first_apply, second_apply], axis=1)


def ahead(x, axis, size):
    return [x, shift(x, axis, size, -1), shift(x, axis, size, 2), shift(x, axis, size, 1)]


def per_device(eigvecs, reflectors, factors, frequencies, region_blocks):
    z, xh, xl, y, k = (lax.axis_index(a) for a in ALL)
    local_blocks = eigvecs.shape[0] // BLOCK
    index = region_blocks - (z * NX + xh) * local_blocks
    coords = jnp.stack([z, xh, xl, y, k]).astype(jnp.int32)
    keep, *sends, own, turned, refl = head(index, coords, eigvecs, reflectors)
    rows = own.shape[0]

    turned = lax.ppermute(turned, ALL, turn_pairs())
    both = keep
    for n, send in enumerate(sends):
        both = both + shift(send, "z", NZ, n + 1)
    cross = both[64:]
    half = [
        jnp.concatenate(
            [lax.dynamic_slice_in_dim(both, which * 32, 32, 0), cross], axis=0
        )
        for which in (xh, 1 - xh)
    ]
    both = half[0] + flip(half[1], "xh", NX, 1)
    p = apply_factors(both, factors)
    p = jnp.concatenate([p, flip(p, "xh", NX, 1)], axis=0)
    across = flip(own, "xl", NL, 1)
    p, turned = lax.optimization_barrier((p, turned))
    p = jnp.concatenate([p, flip(p, "xl", NL, 1)], axis=0)
    p = ahead(p, "z", NZ)

    a, b = {}, {}
    b[0] = jnp.concatenate([turned, flip(turned, "xh", NX, 1)], axis=0)
    a[0] = jnp.concatenate(
        [own] + [v[:64] for v in p] + [across] + [v[64:] for v in p], axis=0
    )
    size_a, size_b = rows + 256, turned.shape[0]
    b[1] = shift(b[0], "z", NZ, -1)
    b[3] = shift(b[0], "z", NZ, 1)
    a[1] = shift(a[0], "y", NY, -1)
    a[3] = shift(a[0], "y", NY, 1)
    b2 = [shift(b[1][:size_b], "z", NZ, -1), shift(b[3][size_b:], "z", NZ, 1)]
    a2 = [shift(a[1][:size_a], "y", NY, -1), shift(a[3][size_a:], "y", NY, 1)]

    a_list, b_list = [], []
    for n in range(2):
        a_list += [(n * NY + d, (n * size_a, size_a), v) for d, v in a.items()]
        a_list += [(n * NY + 2, (0, size_a), a2[n])]
        b_list += [((n, d), (n * size_b, size_b), v) for d, v in b.items()]
        b_list += [((n, 2), (0, size_b), b2[n])]
    return final(coords, frequencies.reshape(-1, 128), refl, a_list, b_list)


def solution(mesh):
    grid = Mesh(mesh.devices.reshape(NZ, NX, NL, NY, NC), ALL)
    row, col = ("z", "xh"), ("xl", "y", "core")
    return jax.shard_map(
        per_device,
        mesh=grid,
        in_specs=(P(row, col), P(None, row, None), P(), P(), P(row)),
        out_specs=P(row, col),
        check_vma=False,
    )
```

```python
import jax
import jax.numpy as jnp
from jax import lax
from jax.experimental import pallas as pl
from jax.experimental.pallas import tpu as pltpu
from jax.sharding import Mesh, PartitionSpec as P

BLOCK = 128
F32 = jnp.float32
BF16 = jnp.bfloat16
ALL = ("z", "xh", "xl", "y", "core")
NZ, NX, NL, NY, NC = 4, 2, 2, 4, 2


def shift(x, axis, size, step):
    return lax.ppermute(x, axis, [(i, (i + step) % size) for i in range(size)])


def flip(x, axis, size, bit):
    return lax.ppermute(x, axis, [(i, i ^ bit) for i in range(size)])


def place(z, xh, xl, y, k):
    return (((z * NX + xh) * NL + xl) * NY + y) * NC + k


def turn_pairs():
    pairs = []
    for z in range(NZ):
        for xh in range(NX):
            for xl in range(NL):
                for y in range(NY):
                    turn = 2 * (z & 1) + xh
                    to = (
                        (z - y + turn) % NZ,
                        xh ^ xl ^ (z >> 1) ^ (y & 1),
                        z >> 1,
                        turn,
                    )
                    for k in range(NC):
                        pairs.append((place(z, xh, xl, y, k), place(*to, k)))
    return pairs


def first_dims(left, right):
    return lax.dot_general(
        left, right, (((0,), (0,)), ((), ())), preferred_element_type=F32
    )


def last_dims(left, right):
    return lax.dot_general(
        left, right, (((1,), (1,)), ((), ())), preferred_element_type=F32
    )


def last_dims_exact(left, right):
    return lax.dot_general(
        left,
        right,
        (((1,), (1,)), ((), ())),
        precision=lax.Precision.HIGHEST,
        preferred_element_type=F32,
    )


STEPS = 4


def head_kernel(
    index,
    coords,
    vecs_block,
    refl_block,
    eigvecs,
    reflectors,
    keep,
    send_1,
    send_2,
    send_3,
    own,
    turned,
    refl,
    sums,
    cross,
    sem,
    sem_refl,
):
    step = pl.program_id(0)
    rows, width = own.shape[0], reflectors.shape[2]
    share = turned.shape[0] - rows
    copies, copies_refl = [], []
    for i in range(rows // BLOCK):
        take = pl.ds(pl.multiple_of(index[i] * BLOCK, BLOCK), BLOCK)
        to = pl.ds(i * BLOCK, BLOCK)
        for n, out in enumerate((own, turned)):
            copies.append(
                pltpu.make_async_copy(eigvecs.at[take], out.at[to], sem.at[2 * i + n])
            )
        for n in range(2):
            copies_refl.append(
                pltpu.make_async_copy(
                    reflectors.at[n, take],
                    refl.at[to, pl.ds(n * width, width)],
                    sem_refl.at[2 * i + n],
                )
            )

    @pl.when(step == 0)
    def _():
        for copy in copies_refl + copies:
            copy.start()
        sums[...] = jnp.zeros_like(sums)
        cross[...] = jnp.zeros_like(cross)

    both = jnp.concatenate([refl_block[0], refl_block[1]], axis=1)
    sums[...] += first_dims(vecs_block[...], both)
    cross[...] += first_dims(refl_block[1], refl_block[0])

    @pl.when(step == STEPS - 1)
    def _():
        part = sums.shape[0] // NZ
        wide = jnp.concatenate([cross[:part, :], cross[part:, :]], axis=1)
        for n, out in enumerate((keep, send_1, send_2, send_3)):
            to = lax.rem(coords[0] + n, NZ)
            out[:part, :] = sums[pl.ds(pl.multiple_of(to * part, part), part), :]
            out[part:, :] = wide
        for copy in copies_refl:
            copy.wait()
        start = pl.multiple_of((coords[2] * NY + coords[3]) * share, 16)
        for copy in copies:
            copy.wait()
        turned[rows:, :] = refl[pl.ds(start, share), :]


def head(index, coords, eigvecs, reflectors):
    rows = index.shape[0] * BLOCK
    local, columns = eigvecs.shape
    width = reflectors.shape[2]
    block = local // STEPS
    smem = pl.BlockSpec(memory_space=pltpu.SMEM)
    vmem = pl.BlockSpec(memory_space=pltpu.VMEM)
    hbm = pl.BlockSpec(memory_space=pltpu.HBM)
    sums = jax.ShapeDtypeStruct((128, 256), F32)
    return pl.pallas_call(
        head_kernel,
        grid=(STEPS,),
        in_specs=[
            smem,
            smem,
            pl.BlockSpec((block, columns), lambda i: (i, 0)),
            pl.BlockSpec((2, block, width), lambda i: (0, i, 0)),
            hbm,
            hbm,
        ],
        out_specs=[vmem] * 7,
        out_shape=[sums] * 4
        + [
            jax.ShapeDtypeStruct((rows, columns), BF16),
            jax.ShapeDtypeStruct((rows + rows // 8, columns), BF16),
            jax.ShapeDtypeStruct((rows, 2 * width), BF16),
        ],
        scratch_shapes=[
            pltpu.VMEM((256, 256), F32),
            pltpu.VMEM((128, 128), F32),
            pltpu.SemaphoreType.DMA((2 * index.shape[0],)),
            pltpu.SemaphoreType.DMA((2 * index.shape[0],)),
        ],
        compiler_params=pltpu.CompilerParams(vmem_limit_bytes=20 * 2**20),
        name="head",
    )(
        index,
        coords,
        *[pltpu.with_memory_space_constraint(v, pltpu.HBM) for v in (eigvecs, reflectors)] * 2,
    )


def source_of(z, xh, xl, y, dxh, dz):
    zz = lax.rem(z + dz, NZ)
    from_y = lax.rem(2 * xl + (y >> 1) + y - zz + NZ, NZ)
    from_l = (xh + dxh + (y & 1) + xl + (from_y & 1)) & 1
    return from_y, from_l


def weigh(freqs):
    return 1.0 / jnp.tanh(freqs / 2.0) / (2.0 * freqs)


def final_kernel(slots_a, slots_b, coords, freqs, ya, *rest):
    p_refs, rest = rest[:NY], rest[NY:]
    a_refs, rest = rest[: len(slots_a)], rest[len(slots_a) :]
    b_refs, rest = rest[: len(slots_b)], rest[len(slots_b) :]
    c_other, c_own, a_all, b_all, yb, p_all = rest
    z, xh, xl, y, k = (coords[i] for i in range(5))
    rows = ya.shape[0]
    share = rows // 8

    for dy, p_ref in enumerate(p_refs):
        for dx in range(NL):
            for dxh in range(NX):
                for dz in range(NZ):
                    zz = lax.rem(z + dz, NZ)
                    xx = jnp.bitwise_xor(xh, dxh)
                    slot = dx * NY + dy
                    to = pl.multiple_of(slot * 256 + (zz * NX + xx) * 32, 32)
                    chunk = ((dx * NX + dxh) * NZ + dz) * 32
                    p_all[pl.ds(to, 32), :] = p_ref[chunk : chunk + 32, :]
    for ((dxh, dz), (first, _)), ref in zip(slots_b, b_refs):
        from_y, from_l = source_of(z, xh, xl, y, dxh, dz)
        to = pl.multiple_of((from_l * NY + from_y) * share, 16)
        yb[pl.ds(to, share), :] = ref[first + rows : first + rows + share, :]

    for ((dxh, dz), (first, _)), ref in zip(slots_b, b_refs):
        from_y, from_l = source_of(z, xh, xl, y, dxh, dz)
        dx = jnp.bitwise_xor(from_l, xl)
        slot = dx * NY + lax.rem(from_y - y + NY, NY)
        whole = (from_l * NY + from_y) * NC + k
        at = pl.multiple_of(slot * 256, 256)
        value = ref[first : first + rows, :].astype(F32) - last_dims(
            yb[...], p_all[pl.ds(at, 256), :]
        )
        value = value * weigh(
            jnp.concatenate(
                [freqs[pl.ds(2 * whole, 1), :], freqs[pl.ds(2 * whole + 1, 1), :]],
                axis=1,
            )
        )
        b_all[:, pl.ds(at, 256)] = value.astype(BF16)
    for (slot, (first, _)), ref in zip(slots_a, a_refs):
        cols = slice(slot * 256, slot * 256 + 256)
        value = ref[first : first + rows, :].astype(F32) - last_dims(
            ya[...], p_all[cols, :]
        )
        a_all[:, cols] = value.astype(BF16)
    half = c_own.shape[0]

    def product(which):
        return last_dims(
            b_all[pl.ds(pl.multiple_of(which * half, half), half), :], a_all[...]
        )

    c_other[...] = product(1 - k).astype(BF16)
    c_own[...] = product(k)


def add_kernel(own, other, out):
    rows = out.shape[0]
    at = pl.ds(pl.multiple_of(pl.program_id(0) * rows, rows), rows)
    out[...] = own[at, :] + other[at, :].astype(F32)


def final(coords, freqs, ya, p_list, a_list, b_list):
    slots_a = [(s, take) for s, take, _ in a_list]
    slots_b = [(s, take) for s, take, _ in b_list]
    smem = pl.BlockSpec(memory_space=pltpu.SMEM)
    vmem = pl.BlockSpec(memory_space=pltpu.VMEM)
    rows = ya.shape[0]
    half = rows // 2
    depth = 256 * NL * NY

    def body(*refs):
        final_kernel(slots_a, slots_b, *refs)

    other, own = pl.pallas_call(
        body,
        out_shape=[
            jax.ShapeDtypeStruct((half, rows), BF16),
            jax.ShapeDtypeStruct((half, rows), F32),
        ],
        in_specs=[smem] + [vmem] * (2 + NY + len(a_list) + len(b_list)),
        out_specs=[vmem, vmem],
        scratch_shapes=[
            pltpu.VMEM((rows, depth), BF16),
            pltpu.VMEM((rows, depth), BF16),
            pltpu.VMEM((rows, 256), BF16),
            pltpu.VMEM((depth, 256), BF16),
        ],
        compiler_params=pltpu.CompilerParams(vmem_limit_bytes=24 * 2**20),
        name="covariance",
    )(coords, freqs, ya, *p_list, *[v for _, _, v in a_list], *[v for _, _, v in b_list])
    got = flip(other, "core", NC, 1)
    return pl.pallas_call(
        add_kernel,
        grid=(4,),
        in_specs=[vmem, vmem],
        out_specs=pl.BlockSpec((half // 4, rows), lambda i: (i, 0)),
        out_shape=jax.ShapeDtypeStruct((half, rows), F32),
        compiler_params=pltpu.CompilerParams(vmem_limit_bytes=4 * 2**20),
        name="add",
    )(own, got).T


def apply_factors(both, factors):
    part, cross = both[:32], both[32:]
    cross = jnp.concatenate([cross[:, :128], cross[:, 128:]], axis=0)
    t1, t2 = jnp.triu(factors[0]), jnp.triu(factors[1])
    second_apply = last_dims_exact(part[:, 128:], t2).astype(BF16)
    first_part = part[:, :128] - jnp.dot(
        second_apply.astype(F32), cross, precision=lax.Precision.HIGHEST
    )
    first_apply = last_dims_exact(first_part, t1).astype(BF16)
    return jnp.concatenate([first_apply, second_apply], axis=1)


def ahead(x, axis, size):
    return [x, shift(x, axis, size, -1), shift(x, axis, size, 2), shift(x, axis, size, 1)]


def per_device(eigvecs, reflectors, factors, frequencies, region_blocks):
    z, xh, xl, y, k = (lax.axis_index(a) for a in ALL)
    local_blocks = eigvecs.shape[0] // BLOCK
    index = region_blocks - (z * NX + xh) * local_blocks
    coords = jnp.stack([z, xh, xl, y, k]).astype(jnp.int32)
    keep, *sends, own, turned, refl = head(index, coords, eigvecs, reflectors)
    rows = own.shape[0]

    together = lax.optimization_barrier
    both = keep
    for n, send in enumerate(sends):
        both = both + shift(send, "z", NZ, n + 1)
    turned = lax.ppermute(turned, ALL, turn_pairs())
    across = flip(own, "xl", NL, 1)

    cross = both[64:]
    half = [
        jnp.concatenate(
            [lax.dynamic_slice_in_dim(both, which * 32, 32, 0), cross], axis=0
        )
        for which in (xh, 1 - xh)
    ]
    both = half[0] + flip(half[1], "xh", NX, 1)

    a, b = {}, {}
    a[0] = jnp.concatenate([own, across], axis=0)
    both, turned, a[0] = together((both, turned, a[0]))
    b[0] = jnp.concatenate([turned, flip(turned, "xh", NX, 1)], axis=0)
    a[1] = shift(a[0], "y", NY, -1)
    a[3] = shift(a[0], "y", NY, 1)
    p = apply_factors(both, factors)
    p = jnp.concatenate(ahead(p, "z", NZ), axis=0)

    p, b[0] = together((p, b[0]))
    size_a, size_b = rows, turned.shape[0]
    b[1] = shift(b[0], "z", NZ, -1)
    b[3] = shift(b[0], "z", NZ, 1)
    p, a[1], a[3] = together((p, a[1], a[3]))
    p = jnp.concatenate([p, flip(p, "xh", NX, 1)], axis=0)
    p = jnp.concatenate([p, flip(p, "xl", NL, 1)], axis=0)
    p_list = ahead(p, "y", NY)
    a[1], a[3], *p_list = together((a[1], a[3], *p_list))
    a2 = [shift(a[1][:size_a], "y", NY, -1), shift(a[3][size_a:], "y", NY, 1)]
    b2 = [shift(b[1][:size_b], "z", NZ, -1), shift(b[3][size_b:], "z", NZ, 1)]

    a_list, b_list = [], []
    for n in range(2):
        a_list += [(n * NY + d, (n * size_a, size_a), v) for d, v in a.items()]
        a_list += [(n * NY + 2, (0, size_a), a2[n])]
        b_list += [((n, d), (n * size_b, size_b), v) for d, v in b.items()]
        b_list += [((n, 2), (0, size_b), b2[n])]
    return final(coords, frequencies.reshape(-1, 128), refl, p_list, a_list, b_list)


def solution(mesh):
    grid = Mesh(mesh.devices.reshape(NZ, NX, NL, NY, NC), ALL)
    row, col = ("z", "xh"), ("xl", "y", "core")
    return jax.shard_map(
        per_device,
        mesh=grid,
        in_specs=(P(row, col), P(None, row, None), P(), P(), P(row)),
        out_specs=P(row, col),
        check_vma=False,
    )
```

```python
import jax
import jax.numpy as jnp
from jax import lax
from jax.experimental import pallas as pl
from jax.experimental.pallas import tpu as pltpu
from jax.sharding import Mesh, PartitionSpec as P

BLOCK = 128
F32 = jnp.float32
BF16 = jnp.bfloat16
ALL = ("z", "xh", "xl", "y", "core")
NZ, NX, NL, NY, NC = 4, 2, 2, 4, 2


def shift(x, axis, size, step):
    return lax.ppermute(x, axis, [(i, (i + step) % size) for i in range(size)])


def flip(x, axis, size, bit):
    return lax.ppermute(x, axis, [(i, i ^ bit) for i in range(size)])


def place(z, xh, xl, y, k):
    return (((z * NX + xh) * NL + xl) * NY + y) * NC + k


def turn_pairs():
    pairs = []
    for z in range(NZ):
        for xh in range(NX):
            for xl in range(NL):
                for y in range(NY):
                    turn = 2 * (z & 1) + xh
                    to = (
                        (z - y + turn) % NZ,
                        xh ^ xl ^ (z >> 1) ^ (y & 1),
                        z >> 1,
                        turn,
                    )
                    for k in range(NC):
                        pairs.append((place(z, xh, xl, y, k), place(*to, k)))
    return pairs


def first_dims(left, right):
    return lax.dot_general(
        left, right, (((0,), (0,)), ((), ())), preferred_element_type=F32
    )


def last_dims(left, right):
    return lax.dot_general(
        left, right, (((1,), (1,)), ((), ())), preferred_element_type=F32
    )


def last_dims_exact(left, right):
    return lax.dot_general(
        left,
        right,
        (((1,), (1,)), ((), ())),
        precision=lax.Precision.HIGHEST,
        preferred_element_type=F32,
    )


STEPS = 4


def head_kernel(
    index,
    coords,
    vecs_block,
    refl_block,
    eigvecs,
    reflectors,
    keep,
    send_1,
    send_2,
    send_3,
    own,
    turned,
    refl,
    sums,
    cross,
    sem,
    sem_refl,
):
    step = pl.program_id(0)
    rows, width = own.shape[0], reflectors.shape[2]
    share = turned.shape[0] - rows
    copies, copies_refl = [], []
    for i in range(rows // BLOCK):
        take = pl.ds(pl.multiple_of(index[i] * BLOCK, BLOCK), BLOCK)
        to = pl.ds(i * BLOCK, BLOCK)
        for n, out in enumerate((own, turned)):
            copies.append(
                pltpu.make_async_copy(eigvecs.at[take], out.at[to], sem.at[2 * i + n])
            )
        for n in range(2):
            copies_refl.append(
                pltpu.make_async_copy(
                    reflectors.at[n, take],
                    refl.at[to, pl.ds(n * width, width)],
                    sem_refl.at[2 * i + n],
                )
            )

    @pl.when(step == 0)
    def _():
        for copy in copies_refl + copies:
            copy.start()
        sums[...] = jnp.zeros_like(sums)
        cross[...] = jnp.zeros_like(cross)

    both = jnp.concatenate([refl_block[0], refl_block[1]], axis=1)
    sums[...] += first_dims(vecs_block[...], both)
    cross[...] += first_dims(refl_block[1], refl_block[0])

    @pl.when(step == STEPS - 1)
    def _():
        part = sums.shape[0] // NZ
        wide = jnp.concatenate([cross[:part, :], cross[part:, :]], axis=1)
        for n, out in enumerate((keep, send_1, send_2, send_3)):
            to = lax.rem(coords[0] + n, NZ)
            out[:part, :] = sums[pl.ds(pl.multiple_of(to * part, part), part), :]
            out[part:, :] = wide
        for copy in copies_refl:
            copy.wait()
        start = pl.multiple_of((coords[2] * NY + coords[3]) * share, 16)
        for copy in copies:
            copy.wait()
        turned[rows:, :] = refl[pl.ds(start, share), :]


def head(index, coords, eigvecs, reflectors):
    rows = index.shape[0] * BLOCK
    local, columns = eigvecs.shape
    width = reflectors.shape[2]
    block = local // STEPS
    smem = pl.BlockSpec(memory_space=pltpu.SMEM)
    vmem = pl.BlockSpec(memory_space=pltpu.VMEM)
    hbm = pl.BlockSpec(memory_space=pltpu.HBM)
    sums = jax.ShapeDtypeStruct((128, 256), F32)
    return pl.pallas_call(
        head_kernel,
        grid=(STEPS,),
        in_specs=[
            smem,
            smem,
            pl.BlockSpec((block, columns), lambda i: (i, 0)),
            pl.BlockSpec((2, block, width), lambda i: (0, i, 0)),
            hbm,
            hbm,
        ],
        out_specs=[vmem] * 7,
        out_shape=[sums] * 4
        + [
            jax.ShapeDtypeStruct((rows, columns), BF16),
            jax.ShapeDtypeStruct((rows + rows // 8, columns), BF16),
            jax.ShapeDtypeStruct((rows, 2 * width), BF16),
        ],
        scratch_shapes=[
            pltpu.VMEM((256, 256), F32),
            pltpu.VMEM((128, 128), F32),
            pltpu.SemaphoreType.DMA((2 * index.shape[0],)),
            pltpu.SemaphoreType.DMA((2 * index.shape[0],)),
        ],
        compiler_params=pltpu.CompilerParams(vmem_limit_bytes=20 * 2**20),
        name="head",
    )(
        index,
        coords,
        *[pltpu.with_memory_space_constraint(v, pltpu.HBM) for v in (eigvecs, reflectors)] * 2,
    )


def source_of(z, xh, xl, y, dxh, dz):
    zz = lax.rem(z + dz, NZ)
    from_y = lax.rem(2 * xl + (y >> 1) + y - zz + NZ, NZ)
    from_l = (xh + dxh + (y & 1) + xl + (from_y & 1)) & 1
    return from_y, from_l


def weigh(freqs):
    return 1.0 / jnp.tanh(freqs / 2.0) / (2.0 * freqs)


def back(slots_a, a_refs, ya, p_all, a_all):
    rows = ya.shape[0]
    for (slot, (first, _)), ref in zip(slots_a, a_refs):
        cols = slice(slot * 256, slot * 256 + 256)
        value = ref[first : first + rows, :].astype(F32) - last_dims(
            ya[...], p_all[cols, :]
        )
        a_all[:, cols] = value.astype(BF16)


def early_kernel(slots_a, coords, ya, *rest):
    p_refs, rest = rest[:NY], rest[NY:]
    a_refs, (a_all, p_all) = rest[: len(slots_a)], rest[len(slots_a) :]
    z, xh = coords[0], coords[1]
    for dy, p_ref in enumerate(p_refs):
        for dx in range(NL):
            for dxh in range(NX):
                for dz in range(NZ):
                    zz = lax.rem(z + dz, NZ)
                    xx = jnp.bitwise_xor(xh, dxh)
                    slot = dx * NY + dy
                    to = pl.multiple_of(slot * 256 + (zz * NX + xx) * 32, 32)
                    chunk = ((dx * NX + dxh) * NZ + dz) * 32
                    p_all[pl.ds(to, 32), :] = p_ref[chunk : chunk + 32, :]
    back(slots_a, a_refs, ya, p_all, a_all)


def final_kernel(slots_a, slots_b, coords, freqs, ya, p_all, a_early, *rest):
    a_refs, rest = rest[: len(slots_a)], rest[len(slots_a) :]
    b_refs, rest = rest[: len(slots_b)], rest[len(slots_b) :]
    c_other, a_all, b_all, yb = rest
    z, xh, xl, y, k = (coords[i] for i in range(5))
    rows = ya.shape[0]
    share = rows // 8

    for ((dxh, dz), (first, _)), ref in zip(slots_b, b_refs):
        from_y, from_l = source_of(z, xh, xl, y, dxh, dz)
        to = pl.multiple_of((from_l * NY + from_y) * share, 16)
        yb[pl.ds(to, share), :] = ref[first + rows : first + rows + share, :]

    for ((dxh, dz), (first, _)), ref in zip(slots_b, b_refs):
        from_y, from_l = source_of(z, xh, xl, y, dxh, dz)
        dx = jnp.bitwise_xor(from_l, xl)
        slot = dx * NY + lax.rem(from_y - y + NY, NY)
        whole = (from_l * NY + from_y) * NC + k
        at = pl.multiple_of(slot * 256, 256)
        value = ref[first : first + rows, :].astype(F32) - last_dims(
            yb[...], p_all[pl.ds(at, 256), :]
        )
        value = value * weigh(
            jnp.concatenate(
                [freqs[pl.ds(2 * whole, 1), :], freqs[pl.ds(2 * whole + 1, 1), :]],
                axis=1,
            )
        )
        b_all[:, pl.ds(at, 256)] = value.astype(BF16)
    back(slots_a, a_refs, ya, p_all, a_all)
    half = c_other.shape[0]
    which = pl.ds(pl.multiple_of((1 - k) * half, half), half)
    c_other[...] = last_dims(b_all[which, :], a_all[...]).astype(BF16)


def own_kernel(coords, a_all, b_all, c_own):
    half = c_own.shape[0]
    which = pl.ds(pl.multiple_of(coords[4] * half, half), half)
    c_own[...] = last_dims(b_all[which, :], a_all[...])


def add_kernel(own, other, out):
    rows = out.shape[0]
    at = pl.ds(pl.multiple_of(pl.program_id(0) * rows, rows), rows)
    out[...] = own[at, :] + other[at, :].astype(F32)


def final(coords, freqs, ya, p_list, a_list, a_late, b_list):
    slots_a = [(s, take) for s, take, _ in a_list]
    slots_late = [(s, take) for s, take, _ in a_late]
    slots_b = [(s, take) for s, take, _ in b_list]
    smem = pl.BlockSpec(memory_space=pltpu.SMEM)
    vmem = pl.BlockSpec(memory_space=pltpu.VMEM)
    rows = ya.shape[0]
    half = rows // 2
    depth = 256 * NL * NY
    whole = jax.ShapeDtypeStruct((rows, depth), BF16)

    def early(*refs):
        early_kernel(slots_a, *refs)

    a_early, p_all = pl.pallas_call(
        early,
        out_shape=[whole, jax.ShapeDtypeStruct((depth, 256), BF16)],
        in_specs=[smem] + [vmem] * (1 + NY + len(a_list)),
        out_specs=[vmem, vmem],
        compiler_params=pltpu.CompilerParams(vmem_limit_bytes=8 * 2**20),
        name="early",
    )(coords, ya, *p_list, *[v for _, _, v in a_list])

    def body(*refs):
        final_kernel(slots_late, slots_b, *refs)

    other, a_all, b_all = pl.pallas_call(
        body,
        out_shape=[jax.ShapeDtypeStruct((half, rows), BF16), whole, whole],
        in_specs=[smem] + [vmem] * (4 + len(a_late) + len(b_list)),
        out_specs=[vmem] * 3,
        scratch_shapes=[pltpu.VMEM((rows, 256), BF16)],
        input_output_aliases={4: 1},
        compiler_params=pltpu.CompilerParams(vmem_limit_bytes=12 * 2**20),
        name="other_half",
    )(
        coords,
        freqs,
        ya,
        p_all,
        a_early,
        *[v for _, _, v in a_late],
        *[v for _, _, v in b_list],
    )
    own = pl.pallas_call(
        own_kernel,
        out_shape=jax.ShapeDtypeStruct((half, rows), F32),
        in_specs=[smem, vmem, vmem],
        out_specs=vmem,
        compiler_params=pltpu.CompilerParams(vmem_limit_bytes=8 * 2**20),
        name="own_half",
    )(coords, a_all, b_all)
    got = flip(other, "core", NC, 1)
    return pl.pallas_call(
        add_kernel,
        grid=(4,),
        in_specs=[vmem, vmem],
        out_specs=pl.BlockSpec((half // 4, rows), lambda i: (i, 0)),
        out_shape=jax.ShapeDtypeStruct((half, rows), F32),
        compiler_params=pltpu.CompilerParams(vmem_limit_bytes=4 * 2**20),
        name="add",
    )(own, got).T


def apply_factors(both, factors):
    part, cross = both[:32], both[32:]
    cross = jnp.concatenate([cross[:, :128], cross[:, 128:]], axis=0)
    t1, t2 = jnp.triu(factors[0]), jnp.triu(factors[1])
    second_apply = last_dims_exact(part[:, 128:], t2).astype(BF16)
    first_part = part[:, :128] - jnp.dot(
        second_apply.astype(F32), cross, precision=lax.Precision.HIGHEST
    )
    first_apply = last_dims_exact(first_part, t1).astype(BF16)
    return jnp.concatenate([first_apply, second_apply], axis=1)


def ahead(x, axis, size):
    return [x, shift(x, axis, size, -1), shift(x, axis, size, 2), shift(x, axis, size, 1)]


def per_device(eigvecs, reflectors, factors, frequencies, region_blocks):
    z, xh, xl, y, k = (lax.axis_index(a) for a in ALL)
    local_blocks = eigvecs.shape[0] // BLOCK
    index = region_blocks - (z * NX + xh) * local_blocks
    coords = jnp.stack([z, xh, xl, y, k]).astype(jnp.int32)
    keep, *sends, own, turned, refl = head(index, coords, eigvecs, reflectors)
    rows = own.shape[0]

    together = lax.optimization_barrier
    both = keep
    for n, send in enumerate(sends):
        both = both + shift(send, "z", NZ, n + 1)
    turned = lax.ppermute(turned, ALL, turn_pairs())
    across = flip(own, "xl", NL, 1)

    cross = both[64:]
    half = [
        jnp.concatenate(
            [lax.dynamic_slice_in_dim(both, which * 32, 32, 0), cross], axis=0
        )
        for which in (xh, 1 - xh)
    ]
    both = half[0] + flip(half[1], "xh", NX, 1)

    a, b = {}, {}
    a[0] = jnp.concatenate([own, across], axis=0)
    both, turned, a[0] = together((both, turned, a[0]))
    b[0] = jnp.concatenate([turned, flip(turned, "xh", NX, 1)], axis=0)
    a[1] = shift(a[0], "y", NY, -1)
    a[3] = shift(a[0], "y", NY, 1)
    p = apply_factors(both, factors)
    p = jnp.concatenate(ahead(p, "z", NZ), axis=0)

    p, b[0] = together((p, b[0]))
    size_a, size_b = rows, turned.shape[0]
    b[1] = shift(b[0], "z", NZ, -1)
    b[3] = shift(b[0], "z", NZ, 1)
    p, a[1], a[3] = together((p, a[1], a[3]))
    p = jnp.concatenate([p, flip(p, "xh", NX, 1)], axis=0)
    p = jnp.concatenate([p, flip(p, "xl", NL, 1)], axis=0)
    p_list = ahead(p, "y", NY)
    a[1], a[3], *p_list = together((a[1], a[3], *p_list))
    a2 = [shift(a[1][:size_a], "y", NY, -1), shift(a[3][size_a:], "y", NY, 1)]
    b2 = [shift(b[1][:size_b], "z", NZ, -1), shift(b[3][size_b:], "z", NZ, 1)]

    a_list, a_late, b_list = [], [], []
    for n in range(2):
        a_list += [(n * NY + d, (n * size_a, size_a), v) for d, v in a.items()]
        a_late += [(n * NY + 2, (0, size_a), a2[n])]
        b_list += [((n, d), (n * size_b, size_b), v) for d, v in b.items()]
        b_list += [((n, 2), (0, size_b), b2[n])]
    return final(coords, frequencies.reshape(-1, 128), refl, p_list, a_list, a_late, b_list)


def solution(mesh):
    grid = Mesh(mesh.devices.reshape(NZ, NX, NL, NY, NC), ALL)
    row, col = ("z", "xh"), ("xl", "y", "core")
    return jax.shard_map(
        per_device,
        mesh=grid,
        in_specs=(P(row, col), P(None, row, None), P(), P(), P(row)),
        out_specs=P(row, col),
        check_vma=False,
    )
```

```python
import jax
import jax.numpy as jnp
from jax import lax
from jax.experimental import pallas as pl
from jax.experimental.pallas import tpu as pltpu
from jax.sharding import Mesh, PartitionSpec as P

BLOCK = 128
F32 = jnp.float32
BF16 = jnp.bfloat16
ALL = ("z", "xh", "xl", "y", "core")
NZ, NX, NL, NY, NC = 4, 2, 2, 4, 2


def shift(x, axis, size, step):
    return lax.ppermute(x, axis, [(i, (i + step) % size) for i in range(size)])


def flip(x, axis, size, bit):
    return lax.ppermute(x, axis, [(i, i ^ bit) for i in range(size)])


def place(z, xh, xl, y, k):
    return (((z * NX + xh) * NL + xl) * NY + y) * NC + k


def turn_pairs():
    pairs = []
    for z in range(NZ):
        for xh in range(NX):
            for xl in range(NL):
                for y in range(NY):
                    to = ((z + y) % NZ, xh ^ xl ^ (z >> 1), z >> 1, 2 * (z & 1) + xh)
                    for k in range(NC):
                        pairs.append((place(z, xh, xl, y, k), place(*to, k)))
    return pairs


def first_dims(left, right):
    return lax.dot_general(
        left, right, (((0,), (0,)), ((), ())), preferred_element_type=F32
    )


def last_dims(left, right):
    return lax.dot_general(
        left, right, (((1,), (1,)), ((), ())), preferred_element_type=F32
    )


def last_dims_exact(left, right):
    return lax.dot_general(
        left,
        right,
        (((1,), (1,)), ((), ())),
        precision=lax.Precision.HIGHEST,
        preferred_element_type=F32,
    )


STEPS = 4


def head_kernel(
    index,
    coords,
    vecs_block,
    refl_block,
    eigvecs,
    reflectors,
    keep,
    send_1,
    send_2,
    send_3,
    own,
    turned,
    refl,
    sums,
    cross,
    sem,
    sem_refl,
):
    step = pl.program_id(0)
    rows, width = own.shape[0], reflectors.shape[2]
    share = turned.shape[0] - rows
    copies, copies_refl = [], []
    for i in range(rows // BLOCK):
        take = pl.ds(pl.multiple_of(index[i] * BLOCK, BLOCK), BLOCK)
        to = pl.ds(i * BLOCK, BLOCK)
        for n, out in enumerate((own, turned)):
            copies.append(
                pltpu.make_async_copy(eigvecs.at[take], out.at[to], sem.at[2 * i + n])
            )
        for n in range(2):
            copies_refl.append(
                pltpu.make_async_copy(
                    reflectors.at[n, take],
                    refl.at[to, pl.ds(n * width, width)],
                    sem_refl.at[2 * i + n],
                )
            )

    @pl.when(step == 0)
    def _():
        for copy in copies_refl + copies:
            copy.start()
        sums[...] = jnp.zeros_like(sums)
        cross[...] = jnp.zeros_like(cross)

    both = jnp.concatenate([refl_block[0], refl_block[1]], axis=1)
    sums[...] += first_dims(vecs_block[...], both)
    cross[...] += first_dims(refl_block[1], refl_block[0])

    @pl.when(step == STEPS - 1)
    def _():
        part = sums.shape[0] // NZ
        wide = jnp.concatenate([cross[:part, :], cross[part:, :]], axis=1)
        for n, out in enumerate((keep, send_1, send_2, send_3)):
            to = lax.rem(coords[0] + n, NZ)
            out[:part, :] = sums[pl.ds(pl.multiple_of(to * part, part), part), :]
            out[part:, :] = wide
        for copy in copies_refl:
            copy.wait()
        start = pl.multiple_of((coords[2] * NY + coords[3]) * share, 16)
        for copy in copies:
            copy.wait()
        turned[rows:, :] = refl[pl.ds(start, share), :]


def head(index, coords, eigvecs, reflectors):
    rows = index.shape[0] * BLOCK
    local, columns = eigvecs.shape
    width = reflectors.shape[2]
    block = local // STEPS
    smem = pl.BlockSpec(memory_space=pltpu.SMEM)
    vmem = pl.BlockSpec(memory_space=pltpu.VMEM)
    hbm = pl.BlockSpec(memory_space=pltpu.HBM)
    sums = jax.ShapeDtypeStruct((128, 256), F32)
    return pl.pallas_call(
        head_kernel,
        grid=(STEPS,),
        in_specs=[
            smem,
            smem,
            pl.BlockSpec((block, columns), lambda i: (i, 0)),
            pl.BlockSpec((2, block, width), lambda i: (0, i, 0)),
            hbm,
            hbm,
        ],
        out_specs=[vmem] * 7,
        out_shape=[sums] * 4
        + [
            jax.ShapeDtypeStruct((rows, columns), BF16),
            jax.ShapeDtypeStruct((rows + rows // 8, columns), BF16),
            jax.ShapeDtypeStruct((rows, 2 * width), BF16),
        ],
        scratch_shapes=[
            pltpu.VMEM((256, 256), F32),
            pltpu.VMEM((128, 128), F32),
            pltpu.SemaphoreType.DMA((2 * index.shape[0],)),
            pltpu.SemaphoreType.DMA((2 * index.shape[0],)),
        ],
        compiler_params=pltpu.CompilerParams(vmem_limit_bytes=20 * 2**20),
        name="head",
    )(
        index,
        coords,
        *[pltpu.with_memory_space_constraint(v, pltpu.HBM) for v in (eigvecs, reflectors)] * 2,
    )


def source_of(z, xh, xl, y, dxh, dz):
    zz = lax.rem(z + dz, NZ)
    from_y = lax.rem(zz - (2 * xl + (y >> 1)) + NZ, NZ)
    from_l = (xh + dxh + (y & 1) + xl) & 1
    return from_y, from_l


def weigh(freqs):
    return 1.0 / jnp.tanh(freqs / 2.0) / (2.0 * freqs)


def back(slots_a, a_refs, ya, p_all, a_all):
    rows = ya.shape[0]
    for (slot, (first, _)), ref in zip(slots_a, a_refs):
        cols = slice(slot * 256, slot * 256 + 256)
        value = ref[first : first + rows, :].astype(F32) - last_dims(
            ya[...], p_all[cols, :]
        )
        a_all[:, cols] = value.astype(BF16)


def early_kernel(slots_a, coords, ya, *rest):
    p_refs, rest = rest[:NY], rest[NY:]
    a_refs, (a_all, p_all) = rest[: len(slots_a)], rest[len(slots_a) :]
    z, xh = coords[0], coords[1]
    for dy, p_ref in enumerate(p_refs):
        for dx in range(NL):
            for dxh in range(NX):
                for dz in range(NZ):
                    zz = lax.rem(z + dz, NZ)
                    xx = jnp.bitwise_xor(xh, dxh)
                    slot = dx * NY + dy
                    to = pl.multiple_of(slot * 256 + (zz * NX + xx) * 32, 32)
                    chunk = ((dx * NX + dxh) * NZ + dz) * 32
                    p_all[pl.ds(to, 32), :] = p_ref[chunk : chunk + 32, :]
    back(slots_a, a_refs, ya, p_all, a_all)


def final_kernel(slots_a, slots_b, coords, freqs, ya, p_all, a_early, *rest):
    a_refs, rest = rest[: len(slots_a)], rest[len(slots_a) :]
    b_refs, rest = rest[: len(slots_b)], rest[len(slots_b) :]
    c_other, a_all, b_all, yb = rest
    z, xh, xl, y, k = (coords[i] for i in range(5))
    rows = ya.shape[0]
    share = rows // 8

    for ((dxh, dz), (first, _)), ref in zip(slots_b, b_refs):
        from_y, from_l = source_of(z, xh, xl, y, dxh, dz)
        to = pl.multiple_of((from_l * NY + from_y) * share, 16)
        yb[pl.ds(to, share), :] = ref[first + rows : first + rows + share, :]

    for ((dxh, dz), (first, _)), ref in zip(slots_b, b_refs):
        from_y, from_l = source_of(z, xh, xl, y, dxh, dz)
        dx = jnp.bitwise_xor(from_l, xl)
        slot = dx * NY + lax.rem(from_y - y + NY, NY)
        whole = (from_l * NY + from_y) * NC + k
        at = pl.multiple_of(slot * 256, 256)
        value = ref[first : first + rows, :].astype(F32) - last_dims(
            yb[...], p_all[pl.ds(at, 256), :]
        )
        value = value * weigh(
            jnp.concatenate(
                [freqs[pl.ds(2 * whole, 1), :], freqs[pl.ds(2 * whole + 1, 1), :]],
                axis=1,
            )
        )
        b_all[:, pl.ds(at, 256)] = value.astype(BF16)
    back(slots_a, a_refs, ya, p_all, a_all)
    half = c_other.shape[0]
    which = pl.ds(pl.multiple_of((1 - k) * half, half), half)
    c_other[...] = last_dims(b_all[which, :], a_all[...]).astype(BF16)


def own_kernel(coords, a_all, b_all, c_own):
    half = c_own.shape[0]
    which = pl.ds(pl.multiple_of(coords[4] * half, half), half)
    c_own[...] = last_dims(b_all[which, :], a_all[...])


def add_kernel(own, other, out):
    rows = out.shape[0]
    at = pl.ds(pl.multiple_of(pl.program_id(0) * rows, rows), rows)
    out[...] = own[at, :] + other[at, :].astype(F32)


def final(coords, freqs, ya, p_list, a_list, a_late, b_list):
    slots_a = [(s, take) for s, take, _ in a_list]
    slots_late = [(s, take) for s, take, _ in a_late]
    slots_b = [(s, take) for s, take, _ in b_list]
    smem = pl.BlockSpec(memory_space=pltpu.SMEM)
    vmem = pl.BlockSpec(memory_space=pltpu.VMEM)
    rows = ya.shape[0]
    half = rows // 2
    depth = 256 * NL * NY
    whole = jax.ShapeDtypeStruct((rows, depth), BF16)

    def early(*refs):
        early_kernel(slots_a, *refs)

    a_early, p_all = pl.pallas_call(
        early,
        out_shape=[whole, jax.ShapeDtypeStruct((depth, 256), BF16)],
        in_specs=[smem] + [vmem] * (1 + NY + len(a_list)),
        out_specs=[vmem, vmem],
        compiler_params=pltpu.CompilerParams(vmem_limit_bytes=8 * 2**20),
        name="early",
    )(coords, ya, *p_list, *[v for _, _, v in a_list])

    def body(*refs):
        final_kernel(slots_late, slots_b, *refs)

    other, a_all, b_all = pl.pallas_call(
        body,
        out_shape=[jax.ShapeDtypeStruct((half, rows), BF16), whole, whole],
        in_specs=[smem] + [vmem] * (4 + len(a_late) + len(b_list)),
        out_specs=[vmem] * 3,
        scratch_shapes=[pltpu.VMEM((rows, 256), BF16)],
        input_output_aliases={4: 1},
        compiler_params=pltpu.CompilerParams(vmem_limit_bytes=12 * 2**20),
        name="other_half",
    )(
        coords,
        freqs,
        ya,
        p_all,
        a_early,
        *[v for _, _, v in a_late],
        *[v for _, _, v in b_list],
    )
    own = pl.pallas_call(
        own_kernel,
        out_shape=jax.ShapeDtypeStruct((half, rows), F32),
        in_specs=[smem, vmem, vmem],
        out_specs=vmem,
        compiler_params=pltpu.CompilerParams(vmem_limit_bytes=8 * 2**20),
        name="own_half",
    )(coords, a_all, b_all)
    got = flip(other, "core", NC, 1)
    return pl.pallas_call(
        add_kernel,
        grid=(4,),
        in_specs=[vmem, vmem],
        out_specs=pl.BlockSpec((half // 4, rows), lambda i: (i, 0)),
        out_shape=jax.ShapeDtypeStruct((half, rows), F32),
        compiler_params=pltpu.CompilerParams(vmem_limit_bytes=4 * 2**20),
        name="add",
    )(own, got).T


def apply_factors(both, factors):
    part, cross = both[:32], both[32:]
    cross = jnp.concatenate([cross[:, :128], cross[:, 128:]], axis=0)
    t1, t2 = jnp.triu(factors[0]), jnp.triu(factors[1])
    second_apply = last_dims_exact(part[:, 128:], t2).astype(BF16)
    first_part = part[:, :128] - jnp.dot(
        second_apply.astype(F32), cross, precision=lax.Precision.HIGHEST
    )
    first_apply = last_dims_exact(first_part, t1).astype(BF16)
    return jnp.concatenate([first_apply, second_apply], axis=1)


def ahead(x, axis, size):
    return [x, shift(x, axis, size, -1), shift(x, axis, size, 2), shift(x, axis, size, 1)]


def per_device(eigvecs, reflectors, factors, frequencies, region_blocks):
    z, xh, xl, y, k = (lax.axis_index(a) for a in ALL)
    local_blocks = eigvecs.shape[0] // BLOCK
    index = region_blocks - (z * NX + xh) * local_blocks
    coords = jnp.stack([z, xh, xl, y, k]).astype(jnp.int32)
    keep, *sends, own, turned, refl = head(index, coords, eigvecs, reflectors)
    rows = own.shape[0]

    together = lax.optimization_barrier
    both = keep
    for n, send in enumerate(sends):
        both = both + shift(send, "z", NZ, n + 1)
    turned = lax.ppermute(turned, ALL, turn_pairs())
    across = flip(own, "xl", NL, 1)

    cross = both[64:]
    half = [
        jnp.concatenate(
            [lax.dynamic_slice_in_dim(both, which * 32, 32, 0), cross], axis=0
        )
        for which in (xh, 1 - xh)
    ]
    both = half[0] + flip(half[1], "xh", NX, 1)

    a, b = {}, {}
    a[0] = jnp.concatenate([own, across], axis=0)
    both, turned, a[0] = together((both, turned, a[0]))
    b[0] = jnp.concatenate([turned, flip(turned, "xh", NX, 1)], axis=0)
    a[1] = shift(a[0], "y", NY, -1)
    a[3] = shift(a[0], "y", NY, 1)
    p = apply_factors(both, factors)
    p = jnp.concatenate(ahead(p, "z", NZ), axis=0)

    p, b[0] = together((p, b[0]))
    size_a, size_b = rows, turned.shape[0]
    b[1] = shift(b[0], "z", NZ, -1)
    b[3] = shift(b[0], "z", NZ, 1)
    p, a[1], a[3] = together((p, a[1], a[3]))
    p = jnp.concatenate([p, flip(p, "xh", NX, 1)], axis=0)
    p = jnp.concatenate([p, flip(p, "xl", NL, 1)], axis=0)
    p_list = ahead(p, "y", NY)
    a[1], a[3], *p_list = together((a[1], a[3], *p_list))
    a2 = [shift(a[1][:size_a], "y", NY, -1), shift(a[3][size_a:], "y", NY, 1)]
    b2 = [shift(b[1][:size_b], "z", NZ, -1), shift(b[3][size_b:], "z", NZ, 1)]

    a_list, a_late, b_list = [], [], []
    for n in range(2):
        a_list += [(n * NY + d, (n * size_a, size_a), v) for d, v in a.items()]
        a_late += [(n * NY + 2, (0, size_a), a2[n])]
        b_list += [((n, d), (n * size_b, size_b), v) for d, v in b.items()]
        b_list += [((n, 2), (0, size_b), b2[n])]
    return final(coords, frequencies.reshape(-1, 128), refl, p_list, a_list, a_late, b_list)


def solution(mesh):
    grid = Mesh(mesh.devices.reshape(NZ, NX, NL, NY, NC), ALL)
    row, col = ("z", "xh"), ("xl", "y", "core")
    return jax.shard_map(
        per_device,
        mesh=grid,
        in_specs=(P(row, col), P(None, row, None), P(), P(), P(row)),
        out_specs=P(row, col),
        check_vma=False,
    )
```
